32 devices in a mesh: study: 2 (over x), vol: 8 (over z, y), tile: 2 (over core).
Axes of the slice: x: 2, y: 2, z: 4, core: 2. Of those that a mesh axis runs over, the one named last changes fastest.
Arguments:
- spectra: bfloat16 [16, 4, 768, 2048], P(('study', 'vol'), None, 'tile'), parts along dimension 0, may hold values from -6 to 6
- block_scales: float32 [16, 4, 768, 16], P(('study', 'vol'), None, 'tile'), parts along dimension 0, may hold values from 0.3 to 3
- retina_blocks: int32 [12, 2], P(('study', 'tile')), parts along dimension 0, may hold values from 0 to 3, as said below
- quality_block: int32 [16, 6], P(('study', 'vol'), 'tile'), parts along dimension 0, may hold values from 0 to 3, as said below
- quality_bias: float32 [16, 6], P(('study', 'vol'), 'tile'), parts along dimension 0, may hold values from -110 to 160
Outputs:
- angiogram: float32 [1024, 768], P(('study', 'vol'), 'tile'), parts along dimension 0
- joined_structure: float32 [1024, 768], P(('study', 'vol'), 'tile'), parts along dimension 0
- spread_map: float32 [1024, 768], P(('study', 'vol'), 'tile'), parts along dimension 0
The draws below stay inside these ranges and needn't reach their ends.
There are 2 independent parts, one for each index of `study`. The reference program is written for one: setup_inputs(seed, part) draws one part's arguments, and reference() takes and returns one part's arrays. A program takes and returns all parts, laid end to end along the dimension named above; each array names one. Nothing has to cross between parts.
Inputs may be any that keep to these rules, and one draw needn't show every extreme that they name: retina_blocks[j,0] <= retina_blocks[j,1]. quality_block[v,j] lies between retina_blocks[j,0] and retina_blocks[j,1].
All inputs are finite; a program needn't handle non-finite values.
Results may differ from the reference program's by a relative error of at most 0.0015.
Values sent between devices are 32-bit elements; how exact they have to be, the bound alone decides.
A program may use at most 128 MiB of HBM per device.

```python
import math
import jax
import jax.numpy as jnp
from jax import lax

K = 2048
DEPTH = 512
BANDS = 4
REPEATS = 4
DBLK = 128
ABLK = 128
SB = 128
ALINES = 768
VOLS = 8
ABLKS = 6
KB = 16
NDB = 4


def draw_pattern(key):
    key_first = jax.random.fold_in(key, 101)
    key_last = jax.random.fold_in(key, 102)
    key_zero = jax.random.fold_in(key, 103)
    key_top = jax.random.fold_in(key, 104)
    first_block = jax.random.randint(key_first, (ABLKS,), 0, NDB // 2)
    last_block = jax.random.randint(key_last, (ABLKS,), NDB // 2, NDB)
    zero_at = jax.random.randint(key_zero, (), 0, ABLKS)
    top_at = jax.random.randint(key_top, (), 0, ABLKS)
    tile_index = jnp.arange(ABLKS, dtype=jnp.int32)
    first_block = jnp.where(tile_index == zero_at, 0, first_block)
    last_block = jnp.where(tile_index == top_at, NDB - 1, last_block)
    return (first_block.astype(jnp.int32), last_block.astype(jnp.int32), zero_at, top_at)


def draw_retina_blocks(key, part):
    first_block, last_block, zero_at, top_at = draw_pattern(key)
    return jnp.stack([first_block, last_block], axis=1).astype(jnp.int32)


def draw_quality_block(key, part):
    first_block, last_block, zero_at, top_at = draw_pattern(key)
    key_pick = jax.random.fold_in(key, 7)
    key_volume = jax.random.fold_in(key, 8)
    raw_pick = jax.random.randint(key_pick, (VOLS, ABLKS), 0, NDB)
    chosen = first_block[None, :] + raw_pick % (last_block - first_block + 1)[None, :]
    low_volume = jax.random.randint(key_volume, (), 0, VOLS)
    high_volume = (low_volume + 1) % VOLS
    volume_index = jnp.arange(VOLS, dtype=jnp.int32)[:, None]
    tile_index = jnp.arange(ABLKS, dtype=jnp.int32)[None, :]
    chosen = jnp.where((volume_index == low_volume) & (tile_index == zero_at), 0, chosen)
    chosen = jnp.where((volume_index == high_volume) & (tile_index == top_at), NDB - 1, chosen)
    return chosen.astype(jnp.int32)


def draw_quality_bias(key, part):
    return jax.random.uniform(key, (VOLS, ABLKS), jnp.float32, -2.0, 2.0)


def block_scale(rng, dims, shards, least, largest):
    level, own = 1.0, jax.random.fold_in(rng, 6)
    for position, parts in shards:
        draws = jnp.exp(jax.random.uniform(jax.random.fold_in(own, position), (parts,), jnp.float32, least / len(shards), largest / len(shards)))
        level = level * jnp.repeat(draws, dims[position] // parts).reshape([-1 if axis == position else 1 for axis in range(len(dims))])
    return level


def normal_values(own_key, shape, spread, reach, split=(), kind=jnp.bfloat16):
    values = jax.random.normal(own_key, shape, jnp.float32) * spread
    if len(split) > 0:
        values = block_scale(own_key, shape, split, -0.22, 0.18) * values
    return jnp.clip(values, min=-reach, max=reach).astype(kind)


def setup_inputs(seed: int = 0, part: int = 0) -> dict:
    streams_of = jax.random.split(jax.random.key(seed), 6)
    own_keys = jax.random.split(jax.random.fold_in(streams_of[5], part), 6)
    spectra = normal_values(own_keys[0], (VOLS, REPEATS, ALINES, K), 1.0, 6.0, ((0, 8), (2, 2)))
    block_scales = jnp.clip(jnp.exp(math.log(3.0) - 2.3025851 * jax.random.uniform(own_keys[1], (VOLS, REPEATS, ALINES, KB), jnp.float32) ** block_scale(own_keys[1], (VOLS, REPEATS, ALINES, KB), ((0, 8), (2, 2)), -0.2, 0.2)), 0.3, 3.0)
    retina_blocks = draw_retina_blocks(jax.random.fold_in(jax.random.fold_in(streams_of[5], part), 71), part)
    quality_block = draw_quality_block(jax.random.fold_in(jax.random.fold_in(streams_of[5], part), 71), part)
    quality_bias = draw_quality_bias(jax.random.fold_in(jax.random.fold_in(streams_of[5], part), 71), part)
    return {"spectra": spectra, "block_scales": block_scales, "retina_blocks": retina_blocks, "quality_block": quality_block, "quality_bias": quality_bias}


smooth_taps = (1.0 / 9.0, 2.0 / 9.0, 3.0 / 9.0, 2.0 / 9.0, 1.0 / 9.0)

def window_tables():
    sample_index = jnp.arange(K, dtype=jnp.int32)
    depth_index = jnp.arange(DEPTH, dtype=jnp.int32)
    phase_angle = (sample_index[:, None] * depth_index[None, :] % K).astype(jnp.float32) * (2.0 * math.pi / K)
    kernel = jnp.stack([jnp.cos(phase_angle), -jnp.sin(phase_angle)], axis=1)
    centres = (jnp.arange(BANDS, dtype=jnp.float32)[:, None] + 0.5) * (K / BANDS)
    distance = sample_index.astype(jnp.float32)[None, :] - centres
    offsets = distance / (K / 8.0)
    window = jnp.where(jnp.abs(distance) <= K / 2.0, jnp.exp(-0.5 * offsets * offsets), 0.0)
    window = window / jnp.sqrt(lax.optimization_barrier(jnp.sum(window * window, axis=1, keepdims=True)))
    return (window[:, :, None, None] * kernel[None]).astype(jnp.bfloat16)

def spread_columns(values, repeat_width):
    widened = jnp.broadcast_to(values[..., None], values.shape + (repeat_width,))
    return widened.reshape(values.shape[:-1] + (values.shape[-1] * repeat_width,))

def scale_spectra(spectra_vol, scales_vol):
    shaped = spectra_vol.astype(jnp.float32).reshape(scales_vol.shape + (SB,))
    return (shaped * scales_vol[..., None]).reshape(spectra_vol.shape).astype(jnp.bfloat16)

def band_maps(scaled, tables):
    line_count = scaled.shape[1]
    decorrelation = jnp.zeros((DEPTH, line_count), jnp.float32)
    power_total = jnp.zeros((DEPTH, line_count), jnp.float32)
    for band_index in range(BANDS):
        fields = jnp.einsum('kcd,rak->cdra', tables[band_index].astype(jnp.float32), scaled.astype(jnp.float32))
        band_power = fields[0] * fields[0] + fields[1] * fields[1]
        amplitude = jnp.sqrt(band_power + 0.05)
        pair_ratio = 2.0 * amplitude[:, :-1] * amplitude[:, 1:] / (band_power[:, :-1] + band_power[:, 1:] + 0.1)
        decorrelation = decorrelation + lax.optimization_barrier(jnp.sum(1.0 - pair_ratio, axis=1))
        power_total = power_total + lax.optimization_barrier(jnp.sum(band_power, axis=1))
    decorrelation = decorrelation / (BANDS * (REPEATS - 1))
    structure = jnp.log(power_total / (BANDS * REPEATS) + 0.1)
    return (decorrelation, structure)

def retina_mask(first_col, last_col):
    depth_block = jnp.arange(DEPTH, dtype=jnp.int32) // DBLK
    return (depth_block[:, None] >= first_col[None, :]) & (depth_block[:, None] <= last_col[None, :])

def lateral_smooth(padded, line_count):
    filtered = smooth_taps[0] * padded[:, 0:line_count]
    for offset_index in range(1, 5):
        filtered = filtered + smooth_taps[offset_index] * padded[:, offset_index:offset_index + line_count]
    return filtered

def block_quality(structure, qblock):
    tile_count = qblock.shape[0]
    block_means = lax.optimization_barrier(jnp.mean(structure.reshape(NDB, DBLK, tile_count, ABLK), axis=(1, 3)))
    chosen = jnp.arange(NDB, dtype=jnp.int32)[:, None] == qblock[None, :]
    return lax.optimization_barrier(jnp.sum(jnp.where(chosen, block_means, 0.0), axis=0))

def reference(spectra, block_scales, retina_blocks, quality_block, quality_bias):
    tables = window_tables()
    first_col = spread_columns(retina_blocks[:, 0], ABLK)
    last_col = spread_columns(retina_blocks[:, 1], ABLK)
    inside = retina_mask(first_col, last_col)

    def per_volume(volume_items):
        spectra_vol, scales_vol, qblock, bias_row = volume_items
        scaled = scale_spectra(spectra_vol, scales_vol)
        decorrelation, structure = band_maps(scaled, tables)
        masked_decorrelation = jnp.where(inside, decorrelation, 0.0)
        masked_structure = jnp.where(inside, structure, 0.0)
        padded = jnp.pad(masked_decorrelation, ((0, 0), (2, 2)))
        smoothed = lateral_smooth(padded, ALINES)
        volume_score = block_quality(structure, qblock) + bias_row
        return (smoothed, masked_structure, volume_score)
    smoothed, structures, scores = lax.map(per_volume, (spectra, block_scales, quality_block, quality_bias))
    weights = jnp.exp(scores - lax.optimization_barrier(jnp.max(scores, axis=0, keepdims=True)))
    weights = weights / lax.optimization_barrier(jnp.sum(weights, axis=0, keepdims=True))
    column_weights = spread_columns(weights, ABLK)[:, None, :]
    angiogram = lax.optimization_barrier(jnp.sum(column_weights * smoothed, axis=0))
    second_moment = lax.optimization_barrier(jnp.sum(column_weights * smoothed * smoothed, axis=0))
    joined_structure = lax.optimization_barrier(jnp.sum(column_weights * structures, axis=0))
    spread_map = jnp.sqrt(second_moment - angiogram * angiogram + 0.01)
    return (angiogram, joined_structure, spread_map)
```

```python
import functools
import math

import jax
import jax.numpy as jnp
from jax import lax
from jax.experimental import pallas as pl
from jax.experimental.pallas import tpu as pltpu
from jax.sharding import PartitionSpec as P

DEPTH = 512
BANDS = 4
DBLK = 128
ABLK = 128
SB = 128
NDB = 4
CLASSES = 8
MESH = pl.DeviceIdType.MESH
ZR = 136


def build_tables(table, perm, samples):
    inner = samples // CLASSES
    z = lax.broadcasted_iota(jnp.int32, (ZR, inner), 0)
    k1 = lax.broadcasted_iota(jnp.int32, (ZR, inner), 1)
    unit = 2.0 * math.pi / samples
    base = ((CLASSES * k1 * z) % samples).astype(jnp.float32) * unit
    step = z.astype(jnp.float32) * unit
    re, im = jnp.cos(base), -jnp.sin(base)
    sre, sim = jnp.cos(step), -jnp.sin(step)
    kk = (
        lax.broadcasted_iota(jnp.int32, (CLASSES, inner), 1) * CLASSES
        + lax.broadcasted_iota(jnp.int32, (CLASSES, inner), 0)
    ).astype(jnp.float32)
    windows = []
    for b in range(BANDS):
        distance = kk - (b + 0.5) * (samples / BANDS)
        offset = distance / (samples / 8.0)
        g = jnp.where(jnp.abs(distance) <= samples / 2.0, jnp.exp(-0.5 * offset * offset), 0.0)
        windows.append(g / jnp.sqrt(jnp.sum(g * g, keepdims=True)))
    for k0 in range(CLASSES):
        if k0:
            re, im = re * sre - im * sim, re * sim + im * sre
        both = jnp.concatenate([re, im], axis=0)
        for b in range(BANDS):
            row = windows[b][k0 : k0 + 1, :]
            table[k0, b * 2 * ZR : (b + 1) * 2 * ZR, :] = (both * row).astype(jnp.bfloat16)
    size = perm.shape[0]
    part = size // CLASSES
    row = lax.broadcasted_iota(jnp.int32, (size, size), 0)
    col = lax.broadcasted_iota(jnp.int32, (size, size), 1)
    perm[...] = jnp.where(col == (row % part) * CLASSES + row // part, 1.0, 0.0).astype(jnp.bfloat16)


def combine(get):
    rr, ii = [get(k, 0) for k in range(8)], [get(k, 1) for k in range(8)]
    sr = [rr[j] + rr[j + 4] for j in range(4)]
    si = [ii[j] + ii[j + 4] for j in range(4)]
    dr = [rr[j] - rr[j + 4] for j in range(4)]
    di = [ii[j] - ii[j + 4] for j in range(4)]
    half = math.sqrt(0.5)
    re0, im0 = (sr[0] + sr[2]) + (sr[1] + sr[3]), (si[0] + si[2]) + (si[1] + si[3])
    re3, im3 = (sr[0] - sr[2]) - (si[1] - si[3]), (si[0] - si[2]) + (sr[1] - sr[3])
    p, q = (dr[1] - dr[3]) * half, (di[1] + di[3]) * half
    r, t = (di[1] - di[3]) * half, (dr[1] + dr[3]) * half
    re2, im2 = (dr[0] + di[2]) + (p + q), (di[0] - dr[2]) + (r - t)
    re1, im1 = (dr[0] - di[2]) + (p - q), (di[0] + dr[2]) + (r + t)
    fields = ((re0, im0), (re1, im1), (re2, im2), (re3, im3))
    return [re * re + (im * im + 0.05) for re, im in fields]


def compute_kernel(
    retina, qblock, bias, spec, scales, dec_out, str_out, score_out,
    table, perm, data, ga, gb, acc_ratio, acc_power,
):
    j = pl.program_id(0)
    repeats, lines, samples = spec.shape[1:]
    chunk = perm.shape[0]
    part = chunk // CLASSES
    cols = repeats * lines

    @pl.when(j == 0)
    def _():
        build_tables(table, perm, samples)

    scale_t = jnp.concatenate([scales[0, r].T for r in range(repeats)], axis=1)
    for q in range(samples // chunk):
        block = spec[0, :, :, q * chunk : (q + 1) * chunk].reshape(cols, chunk)
        moved = lax.dot_general(
            perm[...], block, (((1,), (1,)), ((), ())), preferred_element_type=jnp.float32
        )
        per = chunk // SB
        factor = jnp.concatenate(
            [
                jnp.broadcast_to(scale_t[q * per + h : q * per + h + 1, :], (part // per, cols))
                for h in range(per)
            ],
            axis=0,
        )
        for k0 in range(CLASSES):
            data[k0, q * part : (q + 1) * part, :] = (
                moved[k0 * part : (k0 + 1) * part] * factor
            ).astype(jnp.bfloat16)

    buffers = (ga, gb)

    def multiply(b):
        for k0 in range(CLASSES):
            buffers[b % 2][k0] = jnp.dot(
                table[k0, b * 2 * ZR : (b + 1) * 2 * ZR, :],
                data[k0],
                preferred_element_type=jnp.float32,
            )

    def reduce(b):
        g = buffers[b % 2]

        for i in range(ZR // 8):
            at = i * 8
            powers = []
            for r in range(repeats):
                def get(k, c):
                    return g[k, c * ZR + at : c * ZR + at + 8, r * lines : (r + 1) * lines]

                powers.append(combine(get))
            for d in range(NDB):
                total = powers[0][d]
                ratio = None
                for r in range(repeats - 1):
                    first, second = powers[r][d], powers[r + 1][d]
                    total = total + second
                    prod, both = first * second, first + second
                    term = prod * lax.rsqrt(prod * (both * both))
                    ratio = term if ratio is None else ratio + term
                if b:
                    total = total + acc_power[d, at : at + 8, :]
                    ratio = ratio + acc_ratio[d, at : at + 8, :]
                acc_power[d, at : at + 8, :] = total
                acc_ratio[d, at : at + 8, :] = ratio

    multiply(0)
    for b in range(BANDS):
        if b + 1 < BANDS:
            multiply(b + 1)
        reduce(b)

    flip = jnp.where(
        lax.broadcasted_iota(jnp.int32, (DBLK, ZR), 0)
        + lax.broadcasted_iota(jnp.int32, (DBLK, ZR), 1)
        == DBLK,
        1.0,
        0.0,
    )
    first, last, rated = retina[j, 0], retina[j, 1], qblock[0, j]
    score = jnp.zeros((1, lines), jnp.float32)
    for d in range(NDB):
        ratio, power = acc_ratio[d], acc_power[d]
        dec = 1.0 - ratio * (2.0 / (BANDS * (repeats - 1)))
        struct = jnp.log(power * (1.0 / (BANDS * repeats)) + 0.05)
        if d % 2:
            dec = jnp.dot(flip, dec, precision=lax.Precision.HIGHEST)
            struct = jnp.dot(flip, struct, precision=lax.Precision.HIGHEST)
        else:
            dec, struct = dec[:DBLK], struct[:DBLK]
        inside = (first <= d) & (d <= last)
        dec_out[d * DBLK : (d + 1) * DBLK, :] = jnp.where(inside, dec, 0.0)
        str_out[d * DBLK : (d + 1) * DBLK, :] = jnp.where(inside, struct, 0.0)
        score = score + jnp.where(rated == d, jnp.sum(struct, axis=0, keepdims=True), 0.0)
    mean = jnp.sum(score, axis=1, keepdims=True) * (1.0 / (DBLK * lines)) + bias[0, j]
    score_out[pl.ds(j, 1), :] = jnp.broadcast_to(mean, (1, score_out.shape[1]))


def compute(spectra, block_scales, retina, qblock, bias):
    _, repeats, lines, samples = spectra.shape
    kb = block_scales.shape[3]
    tiles = lines // ABLK
    inner = samples // CLASSES
    cols = repeats * ABLK
    smem = pl.BlockSpec(memory_space=pltpu.SMEM)
    score_rows = -(-tiles // 8) * 8
    return pl.pallas_call(
        compute_kernel,
        grid=(tiles,),
        out_shape=(
            jax.ShapeDtypeStruct((DEPTH, lines), jnp.float32),
            jax.ShapeDtypeStruct((DEPTH, lines), jnp.float32),
            jax.ShapeDtypeStruct((score_rows, 128), jnp.float32),
        ),
        in_specs=[
            smem, smem, smem,
            pl.BlockSpec((1, repeats, ABLK, samples), lambda j: (0, 0, j, 0)),
            pl.BlockSpec((1, repeats, ABLK, kb), lambda j: (0, 0, j, 0)),
        ],
        out_specs=(
            pl.BlockSpec((DEPTH, ABLK), lambda j: (0, j)),
            pl.BlockSpec((DEPTH, ABLK), lambda j: (0, j)),
            pl.BlockSpec((score_rows, 128), lambda j: (0, 0)),
        ),
        scratch_shapes=[
            pltpu.VMEM((CLASSES, BANDS * 2 * ZR, inner), jnp.bfloat16),
            pltpu.VMEM((256, 256), jnp.bfloat16),
            pltpu.VMEM((CLASSES, inner, cols), jnp.bfloat16),
            pltpu.VMEM((CLASSES, 2 * ZR, cols), jnp.float32),
            pltpu.VMEM((CLASSES, 2 * ZR, cols), jnp.float32),
            pltpu.VMEM((NDB, ZR, ABLK), jnp.float32),
            pltpu.VMEM((NDB, ZR, ABLK), jnp.float32),
        ],
        compiler_params=pltpu.CompilerParams(vmem_limit_bytes=48 * 1024 * 1024),
    )(retina, qblock, bias, spectra, block_scales)


def join_kernel(
    n, dec, struct, score, ang_out, str_out, spread_out,
    rdec, rstr, rscore, redge, ssem, rsem, lsem, esem,
):
    rows = dec.shape[0] // n
    lines = dec.shape[1]
    tiles = lines // ABLK
    me, t = lax.axis_index("vol"), lax.axis_index("tile")
    other = 1 - t
    barrier = pltpu.get_barrier_semaphore()
    for d in range(1, n):
        pl.semaphore_signal(barrier, inc=1, device_id={"vol": (me + d) % n}, device_id_type=MESH)
    pl.semaphore_signal(barrier, inc=1, device_id={"tile": other}, device_id_type=MESH)
    pl.semaphore_wait(barrier, n)

    def pieces(target):
        at = pl.ds(pl.multiple_of(target * rows, 8), rows)
        return (
            (score, rscore.at[me]),
            (dec.at[at, :], rdec.at[me]),
            (struct.at[at, :], rstr.at[me]),
        )

    copies = {}
    for kind in range(3):
        for d in range(1, n):
            target = (me + d) % n
            src, dst = pieces(target)[kind]
            copies[kind, d] = pltpu.make_async_remote_copy(
                src_ref=src, dst_ref=dst, send_sem=ssem.at[kind, d], recv_sem=rsem.at[kind, d],
                device_id={"vol": target}, device_id_type=MESH,
            )
            copies[kind, d].start()
    local = []
    for kind in range(3):
        src, dst = pieces(me)[kind]
        local.append(pltpu.make_async_copy(src, dst, lsem.at[kind]))
        local[-1].start()
    for c in local:
        c.wait()
    for d in range(1, n):
        copies[0, d].wait_recv()
        copies[1, d].wait_recv()
    column = pl.multiple_of((1 - t) * (lines - ABLK), ABLK)
    edge = pltpu.make_async_remote_copy(
        src_ref=rdec.at[:, :, pl.ds(column, ABLK)], dst_ref=redge,
        send_sem=esem.at[0], recv_sem=esem.at[1],
        device_id={"tile": other}, device_id_type=MESH,
    )
    edge.start()
    scores = rscore[...]
    top = jnp.max(scores, axis=0, keepdims=True)
    grown = jnp.exp(scores - top)
    weights = grown / jnp.sum(grown, axis=0, keepdims=True)
    for d in range(1, n):
        copies[2, d].wait_recv()
    edge.wait_recv()
    lane = lax.broadcasted_iota(jnp.int32, (rows, ABLK), 1)
    near = (lane >= t * (ABLK - 2)) & (lane < 2 + t * ABLK)
    width = lines + ABLK
    ang = [jnp.zeros((rows, ABLK), jnp.float32)] * tiles
    square = list(ang)
    joined = list(ang)
    for v in range(n):
        wide = jnp.concatenate([rdec[v], jnp.where(near, redge[v], 0.0)], axis=1)
        smooth = (
            (pltpu.roll(wide, 2, 1) + pltpu.roll(wide, width - 2, 1)) * (1.0 / 9.0)
            + (pltpu.roll(wide, 1, 1) + pltpu.roll(wide, width - 1, 1)) * (2.0 / 9.0)
            + wide * (3.0 / 9.0)
        )
        for j in range(tiles):
            w = weights[v, j : j + 1, :]
            s = smooth[:, j * ABLK : (j + 1) * ABLK]
            ws = w * s
            ang[j] = ang[j] + ws
            square[j] = square[j] + ws * s
            joined[j] = joined[j] + w * rstr[v, :, j * ABLK : (j + 1) * ABLK]
    for j in range(tiles):
        at = slice(j * ABLK, (j + 1) * ABLK)
        ang_out[:, at] = ang[j]
        str_out[:, at] = joined[j]
        spread_out[:, at] = jnp.sqrt(square[j] - ang[j] * ang[j] + 0.01)
    for c in copies.values():
        c.wait_send()
    edge.wait_send()


def join(n, dec, struct, score):
    depth, lines = dec.shape
    rows = depth // n
    vmem = pl.BlockSpec(memory_space=pltpu.VMEM)
    out = jax.ShapeDtypeStruct((rows, lines), jnp.float32)
    return pl.pallas_call(
        functools.partial(join_kernel, n),
        out_shape=(out, out, out),
        in_specs=[vmem] * 3,
        out_specs=(vmem,) * 3,
        scratch_shapes=[
            pltpu.VMEM((n, rows, lines), jnp.float32),
            pltpu.VMEM((n, rows, lines), jnp.float32),
            pltpu.VMEM((n,) + score.shape, jnp.float32),
            pltpu.VMEM((n, rows, ABLK), jnp.float32),
            pltpu.SemaphoreType.DMA((3, n)),
            pltpu.SemaphoreType.DMA((3, n)),
            pltpu.SemaphoreType.DMA((3,)),
            pltpu.SemaphoreType.DMA((2,)),
        ],
        compiler_params=pltpu.CompilerParams(collective_id=0, has_side_effects=True),
    )(dec, struct, score)


def solution(mesh):
    n = mesh.shape["vol"]
    assert mesh.shape["tile"] == 2

    def on_device(spectra, block_scales, retina_blocks, quality_block, quality_bias):
        dec, struct, score = compute(
            spectra, block_scales, retina_blocks, quality_block, quality_bias
        )
        return join(n, dec, struct, score)

    return jax.shard_map(
        on_device,
        mesh=mesh,
        in_specs=(
            P(("study", "vol"), None, "tile", None),
            P(("study", "vol"), None, "tile", None),
            P(("study", "tile"), None),
            P(("study", "vol"), "tile"),
            P(("study", "vol"), "tile"),
        ),
        out_specs=(
            P(("study", "vol"), "tile"),
            P(("study", "vol"), "tile"),
            P(("study", "vol"), "tile"),
        ),
        check_vma=False,
    )
```

```python
import functools
import math

import jax
import jax.numpy as jnp
from jax import lax
from jax.experimental import pallas as pl
from jax.experimental.pallas import tpu as pltpu
from jax.sharding import PartitionSpec as P

DEPTH = 512
BANDS = 4
DBLK = 128
ABLK = 128
SB = 128
NDB = 4
CLASSES = 8
MESH = pl.DeviceIdType.MESH
ZR = 136


def build_tables(table, perm, samples):
    inner = samples // CLASSES
    z = lax.broadcasted_iota(jnp.int32, (ZR, inner), 0)
    k1 = lax.broadcasted_iota(jnp.int32, (ZR, inner), 1)
    unit = 2.0 * math.pi / samples
    base = ((CLASSES * k1 * z) % samples).astype(jnp.float32) * unit
    step = z.astype(jnp.float32) * unit
    re, im = jnp.cos(base), -jnp.sin(base)
    sre, sim = jnp.cos(step), -jnp.sin(step)
    kk = (
        lax.broadcasted_iota(jnp.int32, (CLASSES, inner), 1) * CLASSES
        + lax.broadcasted_iota(jnp.int32, (CLASSES, inner), 0)
    ).astype(jnp.float32)
    windows = []
    for b in range(BANDS):
        distance = kk - (b + 0.5) * (samples / BANDS)
        offset = distance / (samples / 8.0)
        g = jnp.where(jnp.abs(distance) <= samples / 2.0, jnp.exp(-0.5 * offset * offset), 0.0)
        windows.append(g / jnp.sqrt(jnp.sum(g * g, keepdims=True)))
    for k0 in range(CLASSES):
        if k0:
            re, im = re * sre - im * sim, re * sim + im * sre
        both = jnp.concatenate([re, im], axis=0)
        for b in range(BANDS):
            row = windows[b][k0 : k0 + 1, :]
            table[k0, b * 2 * ZR : (b + 1) * 2 * ZR, :] = (both * row).astype(jnp.bfloat16)
    size = perm.shape[0]
    part = size // CLASSES
    row = lax.broadcasted_iota(jnp.int32, (size, size), 0)
    col = lax.broadcasted_iota(jnp.int32, (size, size), 1)
    perm[...] = jnp.where(col == (row % part) * CLASSES + row // part, 1.0, 0.0).astype(jnp.bfloat16)


def combine(get):
    rr, ii = [get(k, 0) for k in range(8)], [get(k, 1) for k in range(8)]
    sr = [rr[j] + rr[j + 4] for j in range(4)]
    si = [ii[j] + ii[j + 4] for j in range(4)]
    dr = [rr[j] - rr[j + 4] for j in range(4)]
    di = [ii[j] - ii[j + 4] for j in range(4)]
    half = math.sqrt(0.5)
    re0, im0 = (sr[0] + sr[2]) + (sr[1] + sr[3]), (si[0] + si[2]) + (si[1] + si[3])
    re3, im3 = (sr[0] - sr[2]) - (si[1] - si[3]), (si[0] - si[2]) + (sr[1] - sr[3])
    p, q = (dr[1] - dr[3]) * half, (di[1] + di[3]) * half
    r, t = (di[1] - di[3]) * half, (dr[1] + dr[3]) * half
    re2, im2 = (dr[0] + di[2]) + (p + q), (di[0] - dr[2]) + (r - t)
    re1, im1 = (dr[0] - di[2]) + (p - q), (di[0] + dr[2]) + (r + t)
    fields = ((re0, im0), (re1, im1), (re2, im2), (re3, im3))
    return [re * re + (im * im + 0.05) for re, im in fields]


def fused_kernel(
    retina, qblock, bias, spec, scales, joined_out,
    table, perm, data, ga, gb, acc_ratio, acc_power,
    sent, got, redge, ssem, rsem, lsem, esem,
):
    j = pl.program_id(0)
    repeats, lines, samples = spec.shape[1:]
    chunk = perm.shape[0]
    tiles, n = sent.shape[:2]
    rows = redge.shape[1]
    me, t = lax.axis_index("vol"), lax.axis_index("tile")
    other = 1 - t
    part = chunk // CLASSES
    cols = repeats * lines

    @pl.when(j == 0)
    def _():
        barrier = pltpu.get_barrier_semaphore()
        for d in range(1, n):
            pl.semaphore_signal(
                barrier, inc=1, device_id={"vol": (me + d) % n}, device_id_type=MESH
            )
        pl.semaphore_signal(barrier, inc=1, device_id={"tile": other}, device_id_type=MESH)
        build_tables(table, perm, samples)

    scale_t = jnp.concatenate([scales[0, r] for r in range(repeats)], axis=1)
    for q in range(samples // chunk):
        block = spec[0, :, :, q * chunk : (q + 1) * chunk].reshape(cols, chunk)
        moved = lax.dot_general(
            perm[...], block, (((1,), (1,)), ((), ())), preferred_element_type=jnp.float32
        )
        per = chunk // SB
        factor = jnp.concatenate(
            [
                jnp.broadcast_to(scale_t[q * per + h : q * per + h + 1, :], (part // per, cols))
                for h in range(per)
            ],
            axis=0,
        )
        for k0 in range(CLASSES):
            data[k0, q * part : (q + 1) * part, :] = (
                moved[k0 * part : (k0 + 1) * part] * factor
            ).astype(jnp.bfloat16)

    buffers = (ga, gb)

    def multiply(b):
        for k0 in range(CLASSES):
            buffers[b % 2][k0] = jnp.dot(
                table[k0, b * 2 * ZR : (b + 1) * 2 * ZR, :],
                data[k0],
                preferred_element_type=jnp.float32,
            )

    def reduce(b):
        g = buffers[b % 2]

        for i in range(ZR // 8):
            at = i * 8
            powers = []
            for r in range(repeats):
                def get(k, c):
                    return g[k, c * ZR + at : c * ZR + at + 8, r * lines : (r + 1) * lines]

                powers.append(combine(get))
            for d in range(NDB):
                total = powers[0][d]
                ratio = None
                for r in range(repeats - 1):
                    first, second = powers[r][d], powers[r + 1][d]
                    total = total + second
                    prod, both = first * second, first + second
                    term = prod * lax.rsqrt(prod * (both * both))
                    ratio = term if ratio is None else ratio + term
                if b:
                    total = total + acc_power[d, at : at + 8, :]
                    ratio = ratio + acc_ratio[d, at : at + 8, :]
                acc_power[d, at : at + 8, :] = total
                acc_ratio[d, at : at + 8, :] = ratio

    multiply(0)
    for b in range(BANDS):
        if b + 1 < BANDS:
            multiply(b + 1)
        reduce(b)

    flip = jnp.where(
        lax.broadcasted_iota(jnp.int32, (DBLK, ZR), 0)
        + lax.broadcasted_iota(jnp.int32, (DBLK, ZR), 1)
        == DBLK,
        1.0,
        0.0,
    )
    first, last, rated = retina[0, j], retina[1, j], qblock[0, j]
    score = jnp.zeros((1, lines), jnp.float32)
    for d in range(NDB):
        ratio, power = acc_ratio[d], acc_power[d]
        dec = 1.0 - ratio * (2.0 / (BANDS * (repeats - 1)))
        struct = jnp.log(power * (1.0 / (BANDS * repeats)) + 0.05)
        if d % 2:
            dec = jnp.dot(flip, dec, precision=lax.Precision.HIGHEST)
            struct = jnp.dot(flip, struct, precision=lax.Precision.HIGHEST)
        else:
            dec, struct = dec[:DBLK], struct[:DBLK]
        inside = (first <= d) & (d <= last)
        score = score + jnp.where(rated == d, jnp.sum(struct, axis=0, keepdims=True), 0.0)
        dec, struct = jnp.where(inside, dec, 0.0), jnp.where(inside, struct, 0.0)
        per = DBLK // rows
        for s in range(per):
            sent[j, d * per + s, :rows, :] = dec[s * rows : (s + 1) * rows]
            sent[j, d * per + s, rows : 2 * rows, :] = struct[s * rows : (s + 1) * rows]
    mean = jnp.sum(score, axis=1, keepdims=True) * (1.0 / (DBLK * lines)) + bias[0, j]
    for u in range(n):
        sent[j, u, 2 * rows :, :] = jnp.broadcast_to(mean, (8, lines))

    def remote(step, d):
        target = (me + d) % n
        return pltpu.make_async_remote_copy(
            src_ref=sent.at[step, target], dst_ref=got.at[step, me],
            send_sem=ssem.at[step, d], recv_sem=rsem.at[step, d],
            device_id={"vol": target}, device_id_type=MESH,
        )

    def local(step):
        return pltpu.make_async_copy(sent.at[step, me], got.at[step, me], lsem.at[step])

    @pl.when(j == 0)
    def _():
        pl.semaphore_wait(pltpu.get_barrier_semaphore(), n)

    for d in range(1, n):
        remote(j, d).start()
    local(j).start()

    @pl.when(j == tiles - 1)
    def _():
        for step in range(tiles):
            local(step).wait()
            for d in range(1, n):
                remote(step, d).wait_recv()
        edge = pltpu.make_async_remote_copy(
            src_ref=got.at[other * (tiles - 1), :, pl.ds(0, rows), :], dst_ref=redge,
            send_sem=esem.at[0], recv_sem=esem.at[1],
            device_id={"tile": other}, device_id_type=MESH,
        )
        edge.start()
        weights = []
        for step in range(tiles):
            scores = [got[step, v, 2 * rows : 2 * rows + 1, :] for v in range(n)]
            top = functools.reduce(jnp.maximum, scores)
            grown = [jnp.exp(x - top) for x in scores]
            total = functools.reduce(jnp.add, grown)
            weights.append([x / total for x in grown])
        for step in range(tiles):
            at = slice(step * lines, (step + 1) * lines)
            total = jnp.zeros((rows, lines), jnp.float32)
            for v in range(n):
                total = total + weights[step][v] * got[step, v, rows : 2 * rows, :]
            joined_out[2, :, at] = total
        lane = lax.broadcasted_iota(jnp.int32, (rows, lines), 1)
        near = (lane >= t * (lines - 2)) & (lane < 2 + t * lines)
        width = (tiles + 1) * lines
        ang = [jnp.zeros((rows, lines), jnp.float32)] * tiles
        square = list(ang)
        edge.wait_recv()
        for v in range(n):
            wide = jnp.concatenate(
                [got[step, v, :rows, :] for step in range(tiles)]
                + [jnp.where(near, redge[v], 0.0)],
                axis=1,
            )
            smooth = (
                (pltpu.roll(wide, 2, 1) + pltpu.roll(wide, width - 2, 1)) * (1.0 / 9.0)
                + (pltpu.roll(wide, 1, 1) + pltpu.roll(wide, width - 1, 1)) * (2.0 / 9.0)
                + wide * (3.0 / 9.0)
            )
            for step in range(tiles):
                w = weights[step][v]
                s = smooth[:, step * lines : (step + 1) * lines]
                ws = w * s
                ang[step] = ang[step] + ws
                square[step] = square[step] + ws * s
        for step in range(tiles):
            at = slice(step * lines, (step + 1) * lines)
            joined_out[0, :, at] = ang[step]
            joined_out[1, :, at] = square[step]
        for step in range(tiles):
            for d in range(1, n):
                remote(step, d).wait_send()
        edge.wait_send()


def fused(n, spectra, block_scales, retina, qblock, bias):
    _, repeats, lines, samples = spectra.shape
    kb = block_scales.shape[3]
    tiles = lines // ABLK
    inner = samples // CLASSES
    cols = repeats * ABLK
    rows = DEPTH // n
    smem = pl.BlockSpec(memory_space=pltpu.SMEM)
    return pl.pallas_call(
        fused_kernel,
        grid=(tiles,),
        out_shape=jax.ShapeDtypeStruct((3, rows, lines), jnp.float32),
        in_specs=[
            smem, smem, smem,
            pl.BlockSpec((1, repeats, ABLK, samples), lambda j: (0, 0, j, 0)),
            pl.BlockSpec((1, repeats, kb, ABLK), lambda j: (0, 0, 0, j)),
        ],
        out_specs=pl.BlockSpec((3, rows, lines), lambda j: (0, 0, 0)),
        scratch_shapes=[
            pltpu.VMEM((CLASSES, BANDS * 2 * ZR, inner), jnp.bfloat16),
            pltpu.VMEM((256, 256), jnp.bfloat16),
            pltpu.VMEM((CLASSES, inner, cols), jnp.bfloat16),
            pltpu.VMEM((CLASSES, 2 * ZR, cols), jnp.float32),
            pltpu.VMEM((CLASSES, 2 * ZR, cols), jnp.float32),
            pltpu.VMEM((NDB, ZR, ABLK), jnp.float32),
            pltpu.VMEM((NDB, ZR, ABLK), jnp.float32),
            pltpu.VMEM((tiles, n, 2 * rows + 8, ABLK), jnp.float32),
            pltpu.VMEM((tiles, n, 2 * rows + 8, ABLK), jnp.float32),
            pltpu.VMEM((n, rows, ABLK), jnp.float32),
            pltpu.SemaphoreType.DMA((tiles, n)),
            pltpu.SemaphoreType.DMA((tiles, n)),
            pltpu.SemaphoreType.DMA((tiles,)),
            pltpu.SemaphoreType.DMA((2,)),
        ],
        compiler_params=pltpu.CompilerParams(
            vmem_limit_bytes=48 * 1024 * 1024, collective_id=0, has_side_effects=True
        ),
    )(retina.T, qblock, bias, spectra, block_scales.transpose(0, 1, 3, 2))


def finish_kernel(joined, ang_out, str_out, spread_out):
    ang = joined[0]
    ang_out[...] = ang
    str_out[...] = joined[2]
    spread_out[...] = jnp.sqrt(joined[1] - ang * ang + 0.01)


def finish(joined):
    out = jax.ShapeDtypeStruct(joined.shape[1:], jnp.float32)
    return pl.pallas_call(finish_kernel, out_shape=(out, out, out))(joined)


def solution(mesh):
    n = mesh.shape["vol"]
    assert mesh.shape["tile"] == 2

    def on_device(spectra, block_scales, retina_blocks, quality_block, quality_bias):
        return finish(
            fused(n, spectra, block_scales, retina_blocks, quality_block, quality_bias)
        )

    return jax.shard_map(
        on_device,
        mesh=mesh,
        in_specs=(
            P(("study", "vol"), None, "tile", None),
            P(("study", "vol"), None, "tile", None),
            P(("study", "tile"), None),
            P(("study", "vol"), "tile"),
            P(("study", "vol"), "tile"),
        ),
        out_specs=(
            P(("study", "vol"), "tile"),
            P(("study", "vol"), "tile"),
            P(("study", "vol"), "tile"),
        ),
        check_vma=False,
    )
```

```python
import functools
import math

import jax
import jax.numpy as jnp
from jax import lax
from jax.experimental import pallas as pl
from jax.experimental.pallas import tpu as pltpu
from jax.sharding import PartitionSpec as P

DEPTH = 512
BANDS = 4
DBLK = 128
ABLK = 128
SB = 128
NDB = 4
CLASSES = 8
MESH = pl.DeviceIdType.MESH
ZR = 136


def build_tables(table, perm, samples):
    inner = samples // CLASSES
    z = lax.broadcasted_iota(jnp.int32, (ZR, inner), 0)
    k1 = lax.broadcasted_iota(jnp.int32, (ZR, inner), 1)
    unit = 2.0 * math.pi / samples
    base = ((CLASSES * k1 * z) % samples).astype(jnp.float32) * unit
    step = z.astype(jnp.float32) * unit
    re, im = jnp.cos(base), -jnp.sin(base)
    sre, sim = jnp.cos(step), -jnp.sin(step)
    kk = (
        lax.broadcasted_iota(jnp.int32, (CLASSES, inner), 1) * CLASSES
        + lax.broadcasted_iota(jnp.int32, (CLASSES, inner), 0)
    ).astype(jnp.float32)
    windows = []
    for b in range(BANDS):
        distance = kk - (b + 0.5) * (samples / BANDS)
        offset = distance / (samples / 8.0)
        g = jnp.where(jnp.abs(distance) <= samples / 2.0, jnp.exp(-0.5 * offset * offset), 0.0)
        windows.append(g / jnp.sqrt(jnp.sum(g * g, keepdims=True)))
    for k0 in range(CLASSES):
        if k0:
            re, im = re * sre - im * sim, re * sim + im * sre
        both = jnp.concatenate([re, im], axis=0)
        for b in range(BANDS):
            row = windows[b][k0 : k0 + 1, :]
            table[k0, b * 2 * ZR : (b + 1) * 2 * ZR, :] = (both * row).astype(jnp.bfloat16)
    size = perm.shape[0]
    part = size // CLASSES
    row = lax.broadcasted_iota(jnp.int32, (size, size), 0)
    col = lax.broadcasted_iota(jnp.int32, (size, size), 1)
    perm[...] = jnp.where(col == (row % part) * CLASSES + row // part, 1.0, 0.0).astype(jnp.bfloat16)


def combine(get):
    rr, ii = [get(k, 0) for k in range(8)], [get(k, 1) for k in range(8)]
    sr = [rr[j] + rr[j + 4] for j in range(4)]
    si = [ii[j] + ii[j + 4] for j in range(4)]
    dr = [rr[j] - rr[j + 4] for j in range(4)]
    di = [ii[j] - ii[j + 4] for j in range(4)]
    half = math.sqrt(0.5)
    re0, im0 = (sr[0] + sr[2]) + (sr[1] + sr[3]), (si[0] + si[2]) + (si[1] + si[3])
    re3, im3 = (sr[0] - sr[2]) - (si[1] - si[3]), (si[0] - si[2]) + (sr[1] - sr[3])
    p, q = (dr[1] - dr[3]) * half, (di[1] + di[3]) * half
    r, t = (di[1] - di[3]) * half, (dr[1] + dr[3]) * half
    re2, im2 = (dr[0] + di[2]) + (p + q), (di[0] - dr[2]) + (r - t)
    re1, im1 = (dr[0] - di[2]) + (p - q), (di[0] + dr[2]) + (r + t)
    fields = ((re0, im0), (re1, im1), (re2, im2), (re3, im3))
    return [re * re + (im * im + 0.05) for re, im in fields]


def fused_kernel(
    retina, qblock, bias, spec, scales, joined_out,
    table, perm, data, ga, gb, acc_ratio, acc_power,
    sent, got, redge, ssem, rsem, lsem, esem,
):
    j = pl.program_id(0)
    repeats, lines, samples = spec.shape[1:]
    chunk = perm.shape[0]
    tiles, n = sent.shape[:2]
    rows = redge.shape[1]
    me, t = lax.axis_index("vol"), lax.axis_index("tile")
    other = 1 - t
    part = chunk // CLASSES
    cols = repeats * lines

    @pl.when(j == 0)
    def _():
        barrier = pltpu.get_barrier_semaphore()
        for d in range(1, n):
            pl.semaphore_signal(
                barrier, inc=1, device_id={"vol": (me + d) % n}, device_id_type=MESH
            )
        pl.semaphore_signal(barrier, inc=1, device_id={"tile": other}, device_id_type=MESH)
        build_tables(table, perm, samples)

    scale_t = jnp.concatenate([scales[0, r] for r in range(repeats)], axis=1)
    for q in range(samples // chunk):
        block = spec[0, :, :, q * chunk : (q + 1) * chunk].reshape(cols, chunk)
        moved = lax.dot_general(
            perm[...], block, (((1,), (1,)), ((), ())), preferred_element_type=jnp.float32
        )
        per = chunk // SB
        factor = jnp.concatenate(
            [
                jnp.broadcast_to(scale_t[q * per + h : q * per + h + 1, :], (part // per, cols))
                for h in range(per)
            ],
            axis=0,
        )
        for k0 in range(CLASSES):
            data[k0, q * part : (q + 1) * part, :] = (
                moved[k0 * part : (k0 + 1) * part] * factor
            ).astype(jnp.bfloat16)

    buffers = (ga, gb)

    def multiply(b):
        for k0 in range(CLASSES):
            buffers[b % 2][k0] = jnp.dot(
                table[k0, b * 2 * ZR : (b + 1) * 2 * ZR, :],
                data[k0],
                preferred_element_type=jnp.float32,
            )

    def reduce(b):
        g = buffers[b % 2]

        for i in range(ZR // 8):
            at = i * 8
            powers = []
            for r in range(repeats):
                def get(k, c):
                    return g[k, c * ZR + at : c * ZR + at + 8, r * lines : (r + 1) * lines]

                powers.append(combine(get))
            for d in range(NDB):
                total = powers[0][d]
                ratio = None
                for r in range(repeats - 1):
                    first, second = powers[r][d], powers[r + 1][d]
                    total = total + second
                    prod, both = first * second, first + second
                    term = prod * lax.rsqrt(prod * (both * both))
                    ratio = term if ratio is None else ratio + term
                if b:
                    total = total + acc_power[d, at : at + 8, :]
                    ratio = ratio + acc_ratio[d, at : at + 8, :]
                acc_power[d, at : at + 8, :] = total
                acc_ratio[d, at : at + 8, :] = ratio

    multiply(0)
    for b in range(BANDS):
        if b + 1 < BANDS:
            multiply(b + 1)
        reduce(b)

    flip = jnp.where(
        lax.broadcasted_iota(jnp.int32, (DBLK, ZR), 0)
        + lax.broadcasted_iota(jnp.int32, (DBLK, ZR), 1)
        == DBLK,
        1.0,
        0.0,
    )
    first, last, rated = retina[0, j], retina[1, j], qblock[0, j]
    score = jnp.zeros((1, lines), jnp.float32)
    for d in range(NDB):
        ratio, power = acc_ratio[d], acc_power[d]
        dec = 1.0 - ratio * (2.0 / (BANDS * (repeats - 1)))
        struct = jnp.log(power * (1.0 / (BANDS * repeats)) + 0.05)
        if d % 2:
            dec = jnp.dot(flip, dec, precision=lax.Precision.HIGHEST)
            struct = jnp.dot(flip, struct, precision=lax.Precision.HIGHEST)
        else:
            dec, struct = dec[:DBLK], struct[:DBLK]
        inside = (first <= d) & (d <= last)
        score = score + jnp.where(rated == d, jnp.sum(struct, axis=0, keepdims=True), 0.0)
        dec, struct = jnp.where(inside, dec, 0.0), jnp.where(inside, struct, 0.0)
        per = DBLK // rows
        for s in range(per):
            sent[j, d * per + s, :rows, :] = dec[s * rows : (s + 1) * rows]
            sent[j, d * per + s, rows : 2 * rows, :] = struct[s * rows : (s + 1) * rows]
    mean = jnp.sum(score, axis=1, keepdims=True) * (1.0 / (DBLK * lines)) + bias[0, j]
    for u in range(n):
        sent[j, u, 2 * rows :, :] = jnp.broadcast_to(mean, (8, lines))

    def remote(step, d):
        target = (me + d) % n
        return pltpu.make_async_remote_copy(
            src_ref=sent.at[step, target], dst_ref=got.at[step, me],
            send_sem=ssem.at[step, d], recv_sem=rsem.at[step, d],
            device_id={"vol": target}, device_id_type=MESH,
        )

    def local(step):
        return pltpu.make_async_copy(sent.at[step, me], got.at[step, me], lsem.at[step])

    @pl.when(j == 0)
    def _():
        pl.semaphore_wait(pltpu.get_barrier_semaphore(), n)

    for d in range(1, n):
        remote(j, d).start()
    local(j).start()

    @pl.when(j == tiles - 1)
    def _():
        for step in range(tiles):
            local(step).wait()
            for d in range(1, n):
                remote(step, d).wait_recv()
        edge = pltpu.make_async_remote_copy(
            src_ref=got.at[other * (tiles - 1), :, pl.ds(0, rows), :], dst_ref=redge,
            send_sem=esem.at[0], recv_sem=esem.at[1],
            device_id={"tile": other}, device_id_type=MESH,
        )
        edge.start()
        weights = []
        for step in range(tiles):
            scores = [got[step, v, 2 * rows : 2 * rows + 1, :] for v in range(n)]
            top = functools.reduce(jnp.maximum, scores)
            grown = [jnp.exp(x - top) for x in scores]
            total = functools.reduce(jnp.add, grown)
            weights.append([x / total for x in grown])
        for step in range(tiles):
            at = slice(step * lines, (step + 1) * lines)
            total = jnp.zeros((rows, lines), jnp.float32)
            for v in range(n):
                total = total + weights[step][v] * got[step, v, rows : 2 * rows, :]
            joined_out[2, :, at] = total
        lane = lax.broadcasted_iota(jnp.int32, (rows, lines), 1)
        near = (lane >= t * (lines - 2)) & (lane < 2 + t * lines)
        width = (tiles + 1) * lines
        ang = [jnp.zeros((rows, lines), jnp.float32)] * tiles
        square = list(ang)
        edge.wait_recv()
        for v in range(n):
            wide = jnp.concatenate(
                [got[step, v, :rows, :] for step in range(tiles)]
                + [jnp.where(near, redge[v], 0.0)],
                axis=1,
            )
            smooth = (
                (pltpu.roll(wide, 2, 1) + pltpu.roll(wide, width - 2, 1)) * (1.0 / 9.0)
                + (pltpu.roll(wide, 1, 1) + pltpu.roll(wide, width - 1, 1)) * (2.0 / 9.0)
                + wide * (3.0 / 9.0)
            )
            for step in range(tiles):
                w = weights[step][v]
                s = smooth[:, step * lines : (step + 1) * lines]
                ws = w * s
                ang[step] = ang[step] + ws
                square[step] = square[step] + ws * s
        for step in range(tiles):
            at = slice(step * lines, (step + 1) * lines)
            joined_out[0, :, at] = ang[step]
            joined_out[1, :, at] = square[step]
        for step in range(tiles):
            for d in range(1, n):
                remote(step, d).wait_send()
        edge.wait_send()


def fused(n, spectra, block_scales, retina, qblock, bias):
    _, repeats, lines, samples = spectra.shape
    kb = block_scales.shape[3]
    tiles = lines // ABLK
    inner = samples // CLASSES
    cols = repeats * ABLK
    rows = DEPTH // n
    smem = pl.BlockSpec(memory_space=pltpu.SMEM)
    return pl.pallas_call(
        fused_kernel,
        grid=(tiles,),
        out_shape=jax.ShapeDtypeStruct((3, rows, lines), jnp.float32),
        in_specs=[
            smem, smem, smem,
            pl.BlockSpec((1, repeats, ABLK, samples), lambda j: (0, 0, j, 0)),
            pl.BlockSpec((1, repeats, kb, ABLK), lambda j: (0, 0, 0, j)),
        ],
        out_specs=pl.BlockSpec((3, rows, lines), lambda j: (0, 0, 0)),
        scratch_shapes=[
            pltpu.VMEM((CLASSES, BANDS * 2 * ZR, inner), jnp.bfloat16),
            pltpu.VMEM((256, 256), jnp.bfloat16),
            pltpu.VMEM((CLASSES, inner, cols), jnp.bfloat16),
            pltpu.VMEM((CLASSES, 2 * ZR, cols), jnp.float32),
            pltpu.VMEM((CLASSES, 2 * ZR, cols), jnp.float32),
            pltpu.VMEM((NDB, ZR, ABLK), jnp.float32),
            pltpu.VMEM((NDB, ZR, ABLK), jnp.float32),
            pltpu.VMEM((tiles, n, 2 * rows + 8, ABLK), jnp.float32),
            pltpu.VMEM((tiles, n, 2 * rows + 8, ABLK), jnp.float32),
            pltpu.VMEM((n, rows, ABLK), jnp.float32),
            pltpu.SemaphoreType.DMA((tiles, n)),
            pltpu.SemaphoreType.DMA((tiles, n)),
            pltpu.SemaphoreType.DMA((tiles,)),
            pltpu.SemaphoreType.DMA((2,)),
        ],
        compiler_params=pltpu.CompilerParams(
            vmem_limit_bytes=67043328, collective_id=0, has_side_effects=True
        ),
    )(retina.T, qblock, bias, spectra, block_scales.transpose(0, 1, 3, 2))


def finish_kernel(joined, ang_out, str_out, spread_out):
    ang = joined[0]
    ang_out[...] = ang
    str_out[...] = joined[2]
    spread_out[...] = jnp.sqrt(joined[1] - ang * ang + 0.01)


def finish(joined):
    out = jax.ShapeDtypeStruct(joined.shape[1:], jnp.float32)
    return pl.pallas_call(finish_kernel, out_shape=(out, out, out))(joined)


def solution(mesh):
    n = mesh.shape["vol"]
    assert mesh.shape["tile"] == 2

    def on_device(spectra, block_scales, retina_blocks, quality_block, quality_bias):
        return finish(
            fused(n, spectra, block_scales, retina_blocks, quality_block, quality_bias)
        )

    return jax.shard_map(
        on_device,
        mesh=mesh,
        in_specs=(
            P(("study", "vol"), None, "tile", None),
            P(("study", "vol"), None, "tile", None),
            P(("study", "tile"), None),
            P(("study", "vol"), "tile"),
            P(("study", "vol"), "tile"),
        ),
        out_specs=(
            P(("study", "vol"), "tile"),
            P(("study", "vol"), "tile"),
            P(("study", "vol"), "tile"),
        ),
        check_vma=False,
    )
```

```python
import functools
import math

import jax
import jax.numpy as jnp
from jax import lax
from jax.experimental import pallas as pl
from jax.experimental.pallas import tpu as pltpu
from jax.sharding import PartitionSpec as P

DEPTH = 512
BANDS = 4
DBLK = 128
ABLK = 128
SB = 128
NDB = 4
CLASSES = 8
MESH = pl.DeviceIdType.MESH
ZR = 136


def build_tables(table, perm, samples):
    inner = samples // CLASSES
    z = lax.broadcasted_iota(jnp.int32, (ZR, inner), 0)
    k1 = lax.broadcasted_iota(jnp.int32, (ZR, inner), 1)
    unit = 2.0 * math.pi / samples
    base = ((CLASSES * k1 * z) % samples).astype(jnp.float32) * unit
    step = z.astype(jnp.float32) * unit
    re, im = jnp.cos(base), -jnp.sin(base)
    sre, sim = jnp.cos(step), -jnp.sin(step)
    kk = (
        lax.broadcasted_iota(jnp.int32, (CLASSES, inner), 1) * CLASSES
        + lax.broadcasted_iota(jnp.int32, (CLASSES, inner), 0)
    ).astype(jnp.float32)
    windows = []
    for b in range(BANDS):
        distance = kk - (b + 0.5) * (samples / BANDS)
        offset = distance / (samples / 8.0)
        g = jnp.where(jnp.abs(distance) <= samples / 2.0, jnp.exp(-0.5 * offset * offset), 0.0)
        windows.append(g / jnp.sqrt(jnp.sum(g * g, keepdims=True)))
    for k0 in range(CLASSES):
        if k0:
            re, im = re * sre - im * sim, re * sim + im * sre
        both = jnp.concatenate([re, im], axis=0)
        for b in range(BANDS):
            row = windows[b][k0 : k0 + 1, :]
            table[k0, b * 2 * ZR : (b + 1) * 2 * ZR, :] = (both * row).astype(jnp.bfloat16)
    size = perm.shape[0]
    part = size // CLASSES
    row = lax.broadcasted_iota(jnp.int32, (size, size), 0)
    col = lax.broadcasted_iota(jnp.int32, (size, size), 1)
    perm[...] = jnp.where(col == (row % part) * CLASSES + row // part, 1.0, 0.0).astype(jnp.bfloat16)


def combine(get):
    rr, ii = [get(k, 0) for k in range(8)], [get(k, 1) for k in range(8)]
    sr = [rr[j] + rr[j + 4] for j in range(4)]
    si = [ii[j] + ii[j + 4] for j in range(4)]
    dr = [rr[j] - rr[j + 4] for j in range(4)]
    di = [ii[j] - ii[j + 4] for j in range(4)]
    half = math.sqrt(0.5)
    re0, im0 = (sr[0] + sr[2]) + (sr[1] + sr[3]), (si[0] + si[2]) + (si[1] + si[3])
    re3, im3 = (sr[0] - sr[2]) - (si[1] - si[3]), (si[0] - si[2]) + (sr[1] - sr[3])
    p, q = (dr[1] - dr[3]) * half, (di[1] + di[3]) * half
    r, t = (di[1] - di[3]) * half, (dr[1] + dr[3]) * half
    re2, im2 = (dr[0] + di[2]) + (p + q), (di[0] - dr[2]) + (r - t)
    re1, im1 = (dr[0] - di[2]) + (p - q), (di[0] + dr[2]) + (r + t)
    fields = ((re0, im0), (re1, im1), (re2, im2), (re3, im3))
    return [re * re + (im * im + 0.05) for re, im in fields]


def fused_kernel(
    retina, qblock, bias, spec, scales, joined_out,
    table, perm, data, ga, gb, acc_ratio, acc_power,
    sent, got, score_sent, score_got, part_sent, part_got, part_near, redge,
    ssem, rsem, csem, dsem, psem, qsem, lsem, esem,
):
    j = pl.program_id(0)
    repeats, lines, samples = spec.shape[1:]
    chunk = perm.shape[0]
    tiles, n = score_got.shape[:2]
    half = n // 2
    rows = redge.shape[2]
    me, t = lax.axis_index("vol"), lax.axis_index("tile")
    other = 1 - t
    side, place = me // half, me % half
    here = tile_at(j, tiles)
    part = chunk // CLASSES
    cols = repeats * lines

    @pl.when(j == 0)
    def _():
        barrier = pltpu.get_barrier_semaphore()
        for d in range(1, n):
            pl.semaphore_signal(
                barrier, inc=1, device_id={"vol": (me + d) % n}, device_id_type=MESH
            )
        pl.semaphore_signal(barrier, inc=1, device_id={"tile": other}, device_id_type=MESH)
        build_tables(table, perm, samples)

    scale_t = jnp.concatenate([scales[0, r] for r in range(repeats)], axis=1)
    for q in range(samples // chunk):
        block = spec[0, :, :, q * chunk : (q + 1) * chunk].reshape(cols, chunk)
        moved = lax.dot_general(
            perm[...], block, (((1,), (1,)), ((), ())), preferred_element_type=jnp.float32
        )
        per = chunk // SB
        factor = jnp.concatenate(
            [
                jnp.broadcast_to(scale_t[q * per + h : q * per + h + 1, :], (part // per, cols))
                for h in range(per)
            ],
            axis=0,
        )
        for k0 in range(CLASSES):
            data[k0, q * part : (q + 1) * part, :] = (
                moved[k0 * part : (k0 + 1) * part] * factor
            ).astype(jnp.bfloat16)

    buffers = (ga, gb)

    def multiply(b):
        for k0 in range(CLASSES):
            buffers[b % 2][k0] = jnp.dot(
                table[k0, b * 2 * ZR : (b + 1) * 2 * ZR, :],
                data[k0],
                preferred_element_type=jnp.float32,
            )

    def reduce(b):
        g = buffers[b % 2]

        for i in range(ZR // 8):
            at = i * 8
            powers = []
            for r in range(repeats):
                def get(k, c):
                    return g[k, c * ZR + at : c * ZR + at + 8, r * lines : (r + 1) * lines]

                powers.append(combine(get))
            for d in range(NDB):
                total = powers[0][d]
                ratio = None
                for r in range(repeats - 1):
                    first, second = powers[r][d], powers[r + 1][d]
                    total = total + second
                    prod, both = first * second, first + second
                    term = prod * lax.rsqrt(prod * (both * both))
                    ratio = term if ratio is None else ratio + term
                if b:
                    total = total + acc_power[d, at : at + 8, :]
                    ratio = ratio + acc_ratio[d, at : at + 8, :]
                acc_power[d, at : at + 8, :] = total
                acc_ratio[d, at : at + 8, :] = ratio

    multiply(0)
    for b in range(BANDS):
        if b + 1 < BANDS:
            multiply(b + 1)
        reduce(b)

    flip = jnp.where(
        lax.broadcasted_iota(jnp.int32, (DBLK, ZR), 0)
        + lax.broadcasted_iota(jnp.int32, (DBLK, ZR), 1)
        == DBLK,
        1.0,
        0.0,
    )
    first, last, rated = retina[0, here], retina[1, here], qblock[0, here]
    score = jnp.zeros((1, lines), jnp.float32)
    for d in range(NDB):
        ratio, power = acc_ratio[d], acc_power[d]
        dec = 1.0 - ratio * (2.0 / (BANDS * (repeats - 1)))
        struct = jnp.log(power * (1.0 / (BANDS * repeats)) + 0.05)
        if d % 2:
            dec = jnp.dot(flip, dec, precision=lax.Precision.HIGHEST)
            struct = jnp.dot(flip, struct, precision=lax.Precision.HIGHEST)
        else:
            dec, struct = dec[:DBLK], struct[:DBLK]
        inside = (first <= d) & (d <= last)
        score = score + jnp.where(rated == d, jnp.sum(struct, axis=0, keepdims=True), 0.0)
        dec, struct = jnp.where(inside, dec, 0.0), jnp.where(inside, struct, 0.0)
        per = DBLK // rows
        for s in range(per):
            u = d * per + s
            sent[j, u % half, u // half, :rows, :] = dec[s * rows : (s + 1) * rows]
            sent[j, u % half, u // half, rows:, :] = struct[s * rows : (s + 1) * rows]
    mean = jnp.sum(score, axis=1, keepdims=True) * (1.0 / (DBLK * lines)) + bias[0, here]
    score_sent[j] = jnp.broadcast_to(mean, (8, lines))

    def maps(step, d):
        target = (place + d) % half
        return pltpu.make_async_remote_copy(
            src_ref=sent.at[step, target], dst_ref=got.at[step, place],
            send_sem=ssem.at[step, d], recv_sem=rsem.at[step, d],
            device_id={"vol": side * half + target}, device_id_type=MESH,
        )

    def scores(step, d):
        return pltpu.make_async_remote_copy(
            src_ref=score_sent.at[step], dst_ref=score_got.at[step, me],
            send_sem=csem.at[step, d], recv_sem=dsem.at[step, d],
            device_id={"vol": (me + d) % n}, device_id_type=MESH,
        )

    def partial(step):
        return pltpu.make_async_remote_copy(
            src_ref=part_sent.at[step], dst_ref=part_got.at[step],
            send_sem=psem.at[step], recv_sem=qsem.at[step],
            device_id={"vol": (1 - side) * half + place}, device_id_type=MESH,
        )

    def own_maps(step):
        return pltpu.make_async_copy(sent.at[step, place], got.at[step, place], lsem.at[0, step])

    def own_score(step):
        return pltpu.make_async_copy(score_sent.at[step], score_got.at[step, me], lsem.at[1, step])

    @pl.when(j == 0)
    def _():
        pl.semaphore_wait(pltpu.get_barrier_semaphore(), n)

    for d in range(1, n):
        scores(j, d).start()
    for d in range(1, half):
        maps(j, d).start()
    own_maps(j).start()
    own_score(j).start()

    @pl.when(j == tiles - 1)
    def _():
        lane = lax.broadcasted_iota(jnp.int32, (rows, lines), 1)
        middle = lines // 2
        inner = (lane >= middle * t) & (lane < middle + middle * t)

        def arrive(step):
            own_maps(step).wait()
            own_score(step).wait()
            for d in range(1, n):
                scores(step, d).wait_recv()
            for d in range(1, half):
                maps(step, d).wait_recv()

        def add_up(step):
            ratings = [score_got[step, v, :1, :] for v in range(n)]
            top = functools.reduce(jnp.maximum, ratings)
            total = functools.reduce(jnp.add, [jnp.exp(x - top) for x in ratings])
            weights = [
                jnp.exp(score_got[step, side * half + v, :1, :] - top) / total
                for v in range(half)
            ]
            for far in range(2):
                to = 1 - side if far else side
                ang = square = joined = jnp.zeros((rows, lines), jnp.float32)
                for v in range(half):
                    own = got[step, v, to, :rows, :]
                    if step + 1 < tiles:
                        after = got[step + 1, v, to, :rows, :]
                    else:
                        after = redge[v, to]
                    before = got[step - 1, v, to, :rows, :] if step else 0.0
                    wide = jnp.concatenate([own, jnp.where(inner, after, before)], axis=1)
                    width = 2 * lines
                    smooth = (
                        (pltpu.roll(wide, 2, 1) + pltpu.roll(wide, width - 2, 1))[:, :lines]
                        * (1.0 / 9.0)
                        + (pltpu.roll(wide, 1, 1) + pltpu.roll(wide, width - 1, 1))[:, :lines]
                        * (2.0 / 9.0)
                        + own * (3.0 / 9.0)
                    )
                    ws = weights[v] * smooth
                    ang = ang + ws
                    square = square + ws * smooth
                    joined = joined + weights[v] * got[step, v, to, rows:, :]
                store = part_sent if far else part_near
                store[step, 0] = ang
                store[step, 1] = square
                store[step, 2] = joined
            partial(step).start()

        edge = pltpu.make_async_remote_copy(
            src_ref=got.at[tiles - 1, :, :, pl.ds(0, rows), :], dst_ref=redge,
            send_sem=esem.at[0], recv_sem=esem.at[1],
            device_id={"tile": other}, device_id_type=MESH,
        )
        arrive(0)
        for step in range(tiles):
            if step + 1 < tiles:
                arrive(step + 1)
            if step + 1 == max(tiles - 1, 1):
                edge.start()
            if step + 1 == tiles:
                edge.wait_recv()
            add_up(step)
        for step in range(tiles):
            partial(step).wait_recv()
            at = pl.ds(pl.multiple_of(tile_at(step, tiles) * lines, lines), lines)
            for k in range(3):
                joined_out[k, :, at] = part_near[step, k] + part_got[step, k]
        for step in range(tiles):
            partial(step).wait_send()
            for d in range(1, n):
                scores(step, d).wait_send()
            for d in range(1, half):
                maps(step, d).wait_send()
        edge.wait_send()


def tile_at(step, tiles):
    t = lax.axis_index("tile")
    return step + t * (tiles - 1 - 2 * step)


def fused(n, spectra, block_scales, retina, qblock, bias):
    _, repeats, lines, samples = spectra.shape
    kb = block_scales.shape[3]
    tiles = lines // ABLK
    inner = samples // CLASSES
    cols = repeats * ABLK
    rows = DEPTH // n
    smem = pl.BlockSpec(memory_space=pltpu.SMEM)
    return pl.pallas_call(
        fused_kernel,
        grid=(tiles,),
        out_shape=jax.ShapeDtypeStruct((3, rows, lines), jnp.float32),
        in_specs=[
            smem, smem, smem,
            pl.BlockSpec((1, repeats, ABLK, samples), lambda j: (0, 0, tile_at(j, tiles), 0)),
            pl.BlockSpec((1, repeats, kb, ABLK), lambda j: (0, 0, 0, tile_at(j, tiles))),
        ],
        out_specs=pl.BlockSpec((3, rows, lines), lambda j: (0, 0, 0)),
        scratch_shapes=[
            pltpu.VMEM((CLASSES, BANDS * 2 * ZR, inner), jnp.bfloat16),
            pltpu.VMEM((256, 256), jnp.bfloat16),
            pltpu.VMEM((CLASSES, inner, cols), jnp.bfloat16),
            pltpu.VMEM((CLASSES, 2 * ZR, cols), jnp.float32),
            pltpu.VMEM((CLASSES, 2 * ZR, cols), jnp.float32),
            pltpu.VMEM((NDB, ZR, ABLK), jnp.float32),
            pltpu.VMEM((NDB, ZR, ABLK), jnp.float32),
            pltpu.VMEM((tiles, n // 2, 2, 2 * rows, ABLK), jnp.float32),
            pltpu.VMEM((tiles, n // 2, 2, 2 * rows, ABLK), jnp.float32),
            pltpu.VMEM((tiles, 8, ABLK), jnp.float32),
            pltpu.VMEM((tiles, n, 8, ABLK), jnp.float32),
            pltpu.VMEM((tiles, 3, rows, ABLK), jnp.float32),
            pltpu.VMEM((tiles, 3, rows, ABLK), jnp.float32),
            pltpu.VMEM((tiles, 3, rows, ABLK), jnp.float32),
            pltpu.VMEM((n // 2, 2, rows, ABLK), jnp.float32),
            pltpu.SemaphoreType.DMA((tiles, n // 2)),
            pltpu.SemaphoreType.DMA((tiles, n // 2)),
            pltpu.SemaphoreType.DMA((tiles, n)),
            pltpu.SemaphoreType.DMA((tiles, n)),
            pltpu.SemaphoreType.DMA((tiles,)),
            pltpu.SemaphoreType.DMA((tiles,)),
            pltpu.SemaphoreType.DMA((2, tiles)),
            pltpu.SemaphoreType.DMA((2,)),
        ],
        compiler_params=pltpu.CompilerParams(
            vmem_limit_bytes=67043328, collective_id=0, has_side_effects=True
        ),
    )(retina.T, qblock, bias, spectra, block_scales.transpose(0, 1, 3, 2))


def finish_kernel(joined, ang_out, str_out, spread_out):
    ang = joined[0]
    ang_out[...] = ang
    str_out[...] = joined[2]
    spread_out[...] = jnp.sqrt(joined[1] - ang * ang + 0.01)


def finish(joined):
    out = jax.ShapeDtypeStruct(joined.shape[1:], jnp.float32)
    return pl.pallas_call(finish_kernel, out_shape=(out, out, out))(joined)


def solution(mesh):
    n = mesh.shape["vol"]
    assert mesh.shape["tile"] == 2

    def on_device(spectra, block_scales, retina_blocks, quality_block, quality_bias):
        return finish(
            fused(n, spectra, block_scales, retina_blocks, quality_block, quality_bias)
        )

    return jax.shard_map(
        on_device,
        mesh=mesh,
        in_specs=(
            P(("study", "vol"), None, "tile", None),
            P(("study", "vol"), None, "tile", None),
            P(("study", "tile"), None),
            P(("study", "vol"), "tile"),
            P(("study", "vol"), "tile"),
        ),
        out_specs=(
            P(("study", "vol"), "tile"),
            P(("study", "vol"), "tile"),
            P(("study", "vol"), "tile"),
        ),
        check_vma=False,
    )
```

```python
import functools
import math

import jax
import jax.numpy as jnp
from jax import lax
from jax.experimental import pallas as pl
from jax.experimental.pallas import tpu as pltpu
from jax.sharding import PartitionSpec as P

DEPTH = 512
BANDS = 4
DBLK = 128
ABLK = 128
SB = 128
NDB = 4
CLASSES = 8
MESH = pl.DeviceIdType.MESH
ZR = 136


def build_tables(table, perm, samples):
    inner = samples // CLASSES
    z = lax.broadcasted_iota(jnp.int32, (ZR, inner), 0)
    k1 = lax.broadcasted_iota(jnp.int32, (ZR, inner), 1)
    unit = 2.0 * math.pi / samples
    base = ((CLASSES * k1 * z) % samples).astype(jnp.float32) * unit
    step = z.astype(jnp.float32) * unit
    re, im = jnp.cos(base), -jnp.sin(base)
    sre, sim = jnp.cos(step), -jnp.sin(step)
    kk = (
        lax.broadcasted_iota(jnp.int32, (CLASSES, inner), 1) * CLASSES
        + lax.broadcasted_iota(jnp.int32, (CLASSES, inner), 0)
    ).astype(jnp.float32)
    windows = []
    for b in range(BANDS):
        distance = kk - (b + 0.5) * (samples / BANDS)
        offset = distance / (samples / 8.0)
        g = jnp.where(jnp.abs(distance) <= samples / 2.0, jnp.exp(-0.5 * offset * offset), 0.0)
        windows.append(g / jnp.sqrt(jnp.sum(g * g, keepdims=True)))
    for k0 in range(CLASSES):
        if k0:
            re, im = re * sre - im * sim, re * sim + im * sre
        both = jnp.concatenate([re, im], axis=0)
        for b in range(BANDS):
            row = windows[b][k0 : k0 + 1, :]
            table[k0, b * 2 * ZR : (b + 1) * 2 * ZR, :] = (both * row).astype(jnp.bfloat16)
    size = perm.shape[0]
    part = size // CLASSES
    row = lax.broadcasted_iota(jnp.int32, (size, size), 0)
    col = lax.broadcasted_iota(jnp.int32, (size, size), 1)
    perm[...] = jnp.where(col == (row % part) * CLASSES + row // part, 1.0, 0.0).astype(jnp.bfloat16)


def combine(get):
    rr, ii = [get(k, 0) for k in range(8)], [get(k, 1) for k in range(8)]
    sr = [rr[j] + rr[j + 4] for j in range(4)]
    si = [ii[j] + ii[j + 4] for j in range(4)]
    dr = [rr[j] - rr[j + 4] for j in range(4)]
    di = [ii[j] - ii[j + 4] for j in range(4)]
    half = math.sqrt(0.5)
    re0, im0 = (sr[0] + sr[2]) + (sr[1] + sr[3]), (si[0] + si[2]) + (si[1] + si[3])
    re3, im3 = (sr[0] - sr[2]) - (si[1] - si[3]), (si[0] - si[2]) + (sr[1] - sr[3])
    p, q = (dr[1] - dr[3]) * half, (di[1] + di[3]) * half
    r, t = (di[1] - di[3]) * half, (dr[1] + dr[3]) * half
    re2, im2 = (dr[0] + di[2]) + (p + q), (di[0] - dr[2]) + (r - t)
    re1, im1 = (dr[0] - di[2]) + (p - q), (di[0] + dr[2]) + (r + t)
    fields = ((re0, im0), (re1, im1), (re2, im2), (re3, im3))
    return [re * re + (im * im + 0.05) for re, im in fields]


def fused_kernel(
    retina, qblock, bias, spec, scales, joined_out,
    table, perm, data, ga, gb, acc_ratio, acc_power,
    sent, got, score_sent, score_got, part_sent, part_got, part_near, redge,
    ssem, rsem, csem, dsem, psem, qsem, lsem, esem,
):
    j = pl.program_id(0)
    repeats, lines, samples = spec.shape[1:]
    chunk = perm.shape[0]
    tiles, n = score_got.shape[:2]
    half = n // 2
    rows = redge.shape[2]
    me, t = lax.axis_index("vol"), lax.axis_index("tile")
    other = 1 - t
    side, place = me // half, me % half
    here = tile_at(j, tiles)
    part = chunk // CLASSES
    cols = repeats * lines

    @pl.when(j == 0)
    def _():
        barrier = pltpu.get_barrier_semaphore()
        for d in range(1, n):
            pl.semaphore_signal(
                barrier, inc=1, device_id={"vol": (me + d) % n}, device_id_type=MESH
            )
        pl.semaphore_signal(barrier, inc=1, device_id={"tile": other}, device_id_type=MESH)
        build_tables(table, perm, samples)

    scale_t = jnp.concatenate([scales[0, r] for r in range(repeats)], axis=1)
    for q in range(samples // chunk):
        block = spec[0, :, :, q * chunk : (q + 1) * chunk].reshape(cols, chunk)
        moved = lax.dot_general(
            perm[...], block, (((1,), (1,)), ((), ())), preferred_element_type=jnp.float32
        )
        per = chunk // SB
        factor = jnp.concatenate(
            [
                jnp.broadcast_to(scale_t[q * per + h : q * per + h + 1, :], (part // per, cols))
                for h in range(per)
            ],
            axis=0,
        )
        for k0 in range(CLASSES):
            data[k0, q * part : (q + 1) * part, :] = (
                moved[k0 * part : (k0 + 1) * part] * factor
            ).astype(jnp.bfloat16)

    buffers = (ga, gb)

    def multiply(b, classes):
        for k0 in classes:
            buffers[b % 2][k0] = jnp.dot(
                table[k0, b * 2 * ZR : (b + 1) * 2 * ZR, :],
                data[k0],
                preferred_element_type=jnp.float32,
            )

    def reduce(b, groups):
        g = buffers[b % 2]

        for i in groups:
            at = i * 8
            powers = []
            for r in range(repeats):
                def get(k, c):
                    return g[k, c * ZR + at : c * ZR + at + 8, r * lines : (r + 1) * lines]

                powers.append(combine(get))
            for d in range(NDB):
                total = powers[0][d]
                ratio = None
                for r in range(repeats - 1):
                    first, second = powers[r][d], powers[r + 1][d]
                    total = total + second
                    prod, both = first * second, first + second
                    term = prod * lax.rsqrt(prod * (both * both))
                    ratio = term if ratio is None else ratio + term
                if b:
                    total = total + acc_power[d, at : at + 8, :]
                    ratio = ratio + acc_ratio[d, at : at + 8, :]
                acc_power[d, at : at + 8, :] = total
                acc_ratio[d, at : at + 8, :] = ratio

    multiply(0, range(CLASSES))
    groups = ZR // 8
    for b in range(BANDS):
        for k0 in range(CLASSES):
            if b + 1 < BANDS:
                multiply(b + 1, (k0,))
            reduce(b, range(k0 * groups // CLASSES, (k0 + 1) * groups // CLASSES))

    flip = jnp.where(
        lax.broadcasted_iota(jnp.int32, (DBLK, ZR), 0)
        + lax.broadcasted_iota(jnp.int32, (DBLK, ZR), 1)
        == DBLK,
        1.0,
        0.0,
    )
    first, last, rated = retina[0, here], retina[1, here], qblock[0, here]
    score = jnp.zeros((1, lines), jnp.float32)
    for d in range(NDB):
        ratio, power = acc_ratio[d], acc_power[d]
        dec = 1.0 - ratio * (2.0 / (BANDS * (repeats - 1)))
        struct = jnp.log(power * (1.0 / (BANDS * repeats)) + 0.05)
        if d % 2:
            dec = jnp.dot(flip, dec, precision=lax.Precision.HIGHEST)
            struct = jnp.dot(flip, struct, precision=lax.Precision.HIGHEST)
        else:
            dec, struct = dec[:DBLK], struct[:DBLK]
        inside = (first <= d) & (d <= last)
        score = score + jnp.where(rated == d, jnp.sum(struct, axis=0, keepdims=True), 0.0)
        dec, struct = jnp.where(inside, dec, 0.0), jnp.where(inside, struct, 0.0)
        per = DBLK // rows
        for s in range(per):
            u = d * per + s
            sent[j, u % half, u // half, :rows, :] = dec[s * rows : (s + 1) * rows]
            sent[j, u % half, u // half, rows:, :] = struct[s * rows : (s + 1) * rows]
    mean = jnp.sum(score, axis=1, keepdims=True) * (1.0 / (DBLK * lines)) + bias[0, here]
    score_sent[j] = jnp.broadcast_to(mean, (8, lines))

    def maps(step, d):
        target = (place + d) % half
        return pltpu.make_async_remote_copy(
            src_ref=sent.at[step, target], dst_ref=got.at[step, place],
            send_sem=ssem.at[step, d], recv_sem=rsem.at[step, d],
            device_id={"vol": side * half + target}, device_id_type=MESH,
        )

    def scores(step, d):
        return pltpu.make_async_remote_copy(
            src_ref=score_sent.at[step], dst_ref=score_got.at[step, me],
            send_sem=csem.at[step, d], recv_sem=dsem.at[step, d],
            device_id={"vol": (me + d) % n}, device_id_type=MESH,
        )

    def partial(step):
        return pltpu.make_async_remote_copy(
            src_ref=part_sent.at[step], dst_ref=part_got.at[step],
            send_sem=psem.at[step], recv_sem=qsem.at[step],
            device_id={"vol": (1 - side) * half + place}, device_id_type=MESH,
        )

    def own_maps(step):
        return pltpu.make_async_copy(sent.at[step, place], got.at[step, place], lsem.at[0, step])

    def own_score(step):
        return pltpu.make_async_copy(score_sent.at[step], score_got.at[step, me], lsem.at[1, step])

    @pl.when(j == 0)
    def _():
        pl.semaphore_wait(pltpu.get_barrier_semaphore(), n)

    for d in range(1, n):
        scores(j, d).start()
    for d in range(1, half):
        maps(j, d).start()
    own_maps(j).start()
    own_score(j).start()

    @pl.when(j == tiles - 1)
    def _():
        lane = lax.broadcasted_iota(jnp.int32, (rows, lines), 1)
        middle = lines // 2
        inner = (lane >= middle * t) & (lane < middle + middle * t)

        def arrive(step):
            own_maps(step).wait()
            own_score(step).wait()
            for d in range(1, n):
                scores(step, d).wait_recv()
            for d in range(1, half):
                maps(step, d).wait_recv()

        def add_up(step):
            ratings = [score_got[step, v, :1, :] for v in range(n)]
            top = functools.reduce(jnp.maximum, ratings)
            total = functools.reduce(jnp.add, [jnp.exp(x - top) for x in ratings])
            weights = [
                jnp.exp(score_got[step, side * half + v, :1, :] - top) / total
                for v in range(half)
            ]
            for far in range(2):
                to = 1 - side if far else side
                ang = square = joined = jnp.zeros((rows, lines), jnp.float32)
                for v in range(half):
                    own = got[step, v, to, :rows, :]
                    if step + 1 < tiles:
                        after = got[step + 1, v, to, :rows, :]
                    else:
                        after = redge[v, to]
                    before = got[step - 1, v, to, :rows, :] if step else 0.0
                    near = jnp.where(inner, after, before)
                    right2 = pltpu.roll(jnp.where(lane >= lines - 2, near, own), 2, 1)
                    right1 = pltpu.roll(jnp.where(lane >= lines - 1, near, own), 1, 1)
                    left1 = pltpu.roll(jnp.where(lane < 1, near, own), lines - 1, 1)
                    left2 = pltpu.roll(jnp.where(lane < 2, near, own), lines - 2, 1)
                    smooth = (
                        (right2 + left2) * (1.0 / 9.0)
                        + (right1 + left1) * (2.0 / 9.0)
                        + own * (3.0 / 9.0)
                    )
                    ws = weights[v] * smooth
                    ang = ang + ws
                    square = square + ws * smooth
                    joined = joined + weights[v] * got[step, v, to, rows:, :]
                store = part_sent if far else part_near
                store[step, 0] = ang
                store[step, 1] = square
                store[step, 2] = joined
            partial(step).start()

        edge = pltpu.make_async_remote_copy(
            src_ref=got.at[tiles - 1, :, :, pl.ds(0, rows), :], dst_ref=redge,
            send_sem=esem.at[0], recv_sem=esem.at[1],
            device_id={"tile": other}, device_id_type=MESH,
        )
        arrive(0)
        for step in range(tiles):
            if step + 1 < tiles:
                arrive(step + 1)
            if step + 1 == max(tiles - 1, 1):
                edge.start()
            if step + 1 == tiles:
                edge.wait_recv()
            add_up(step)
        for step in range(tiles):
            partial(step).wait_recv()
            at = pl.ds(pl.multiple_of(tile_at(step, tiles) * lines, lines), lines)
            for k in range(3):
                joined_out[k, :, at] = part_near[step, k] + part_got[step, k]
        for step in range(tiles):
            partial(step).wait_send()
            for d in range(1, n):
                scores(step, d).wait_send()
            for d in range(1, half):
                maps(step, d).wait_send()
        edge.wait_send()


def tile_at(step, tiles):
    t = lax.axis_index("tile")
    return step + t * (tiles - 1 - 2 * step)


def fused(n, spectra, block_scales, retina, qblock, bias):
    _, repeats, lines, samples = spectra.shape
    kb = block_scales.shape[3]
    tiles = lines // ABLK
    inner = samples // CLASSES
    cols = repeats * ABLK
    rows = DEPTH // n
    smem = pl.BlockSpec(memory_space=pltpu.SMEM)
    return pl.pallas_call(
        fused_kernel,
        grid=(tiles,),
        out_shape=jax.ShapeDtypeStruct((3, rows, lines), jnp.float32),
        in_specs=[
            smem, smem, smem,
            pl.BlockSpec((1, repeats, ABLK, samples), lambda j: (0, 0, tile_at(j, tiles), 0)),
            pl.BlockSpec((1, repeats, kb, ABLK), lambda j: (0, 0, 0, tile_at(j, tiles))),
        ],
        out_specs=pl.BlockSpec((3, rows, lines), lambda j: (0, 0, 0)),
        scratch_shapes=[
            pltpu.VMEM((CLASSES, BANDS * 2 * ZR, inner), jnp.bfloat16),
            pltpu.VMEM((256, 256), jnp.bfloat16),
            pltpu.VMEM((CLASSES, inner, cols), jnp.bfloat16),
            pltpu.VMEM((CLASSES, 2 * ZR, cols), jnp.float32),
            pltpu.VMEM((CLASSES, 2 * ZR, cols), jnp.float32),
            pltpu.VMEM((NDB, ZR, ABLK), jnp.float32),
            pltpu.VMEM((NDB, ZR, ABLK), jnp.float32),
            pltpu.VMEM((tiles, n // 2, 2, 2 * rows, ABLK), jnp.float32),
            pltpu.VMEM((tiles, n // 2, 2, 2 * rows, ABLK), jnp.float32),
            pltpu.VMEM((tiles, 8, ABLK), jnp.float32),
            pltpu.VMEM((tiles, n, 8, ABLK), jnp.float32),
            pltpu.VMEM((tiles, 3, rows, ABLK), jnp.float32),
            pltpu.VMEM((tiles, 3, rows, ABLK), jnp.float32),
            pltpu.VMEM((tiles, 3, rows, ABLK), jnp.float32),
            pltpu.VMEM((n // 2, 2, rows, ABLK), jnp.float32),
            pltpu.SemaphoreType.DMA((tiles, n // 2)),
            pltpu.SemaphoreType.DMA((tiles, n // 2)),
            pltpu.SemaphoreType.DMA((tiles, n)),
            pltpu.SemaphoreType.DMA((tiles, n)),
            pltpu.SemaphoreType.DMA((tiles,)),
            pltpu.SemaphoreType.DMA((tiles,)),
            pltpu.SemaphoreType.DMA((2, tiles)),
            pltpu.SemaphoreType.DMA((2,)),
        ],
        compiler_params=pltpu.CompilerParams(
            vmem_limit_bytes=67043328, collective_id=0, has_side_effects=True
        ),
    )(retina.T, qblock, bias, spectra, block_scales.transpose(0, 1, 3, 2))


def finish_kernel(joined, ang_out, str_out, spread_out):
    ang = joined[0]
    ang_out[...] = ang
    str_out[...] = joined[2]
    spread_out[...] = jnp.sqrt(joined[1] - ang * ang + 0.01)


def finish(joined):
    out = jax.ShapeDtypeStruct(joined.shape[1:], jnp.float32)
    return pl.pallas_call(finish_kernel, out_shape=(out, out, out))(joined)


def solution(mesh):
    n = mesh.shape["vol"]
    assert mesh.shape["tile"] == 2

    def on_device(spectra, block_scales, retina_blocks, quality_block, quality_bias):
        return finish(
            fused(n, spectra, block_scales, retina_blocks, quality_block, quality_bias)
        )

    return jax.shard_map(
        on_device,
        mesh=mesh,
        in_specs=(
            P(("study", "vol"), None, "tile", None),
            P(("study", "vol"), None, "tile", None),
            P(("study", "tile"), None),
            P(("study", "vol"), "tile"),
            P(("study", "vol"), "tile"),
        ),
        out_specs=(
            P(("study", "vol"), "tile"),
            P(("study", "vol"), "tile"),
            P(("study", "vol"), "tile"),
        ),
        check_vma=False,
    )
```
